128 devices in a mesh: rows: 8 (over y_hi, x), feat: 16 (over y_lo, z, core).
Axes of the slice: x: 4, y: 4 (y_hi: 2, y_lo: 2; y = y_hi * 2 + y_lo), z: 4, core: 2. Of those that a mesh axis runs over, the one named last changes fastest.
Arguments:
- bins: int32 [768, 32768], P('feat', 'rows'), may hold values from 0 to 255
- fold: int32 [32768], P('rows'), may hold values from 0 to 9
- nodes: int32 [32768, 10], P('rows'), may hold values from 0 to 3
- gradient: bfloat16 [32768], P('rows'), may hold values from -6 to 6
- hessian: bfloat16 [32768], P('rows'), may hold values from 0.049804688 to 1
Outputs:
- train_hist: float32 [80, 768, 256], P('rows', 'feat')
- node_gain: float32 [10, 4], replicated
The draws below stay inside these ranges and needn't reach their ends.
All inputs are finite; a program needn't handle non-finite values.
Results may differ from the reference program's by a relative error of at most 0.0003.
Values sent between devices are 32-bit elements; how exact they have to be, the bound alone decides.
A program may use at most 64 MiB of HBM per device.

```python
import math
import jax
import jax.numpy as jnp
from jax import lax

F = 768
BINS = 256
FOLDS = 10
NODES = 4
ROWS = 32768


def with_ends(entries, own_key, low, top_value):
    longest = entries.shape.index(max(entries.shape))
    spots = []
    for shift in (0, 1):
        where = [jax.random.randint(jax.random.fold_in(own_key, axis), (), 0, length) for axis, length in enumerate(entries.shape)]
        where[longest] = (where[longest] + shift) % entries.shape[longest]
        spots.append(tuple(where))
    return entries.at[spots[0]].set(low).at[spots[1]].set(top_value)


def block_scale(stream_key, dims, shards, smallest, high):
    loudness, own = 1.0, jax.random.fold_in(stream_key, 6)
    for axis_at, shards_of in shards:
        steps = jnp.exp(jax.random.uniform(jax.random.fold_in(own, axis_at), (shards_of,), jnp.float32, smallest / len(shards), high / len(shards)))
        loudness = loudness * jnp.repeat(steps, dims[axis_at] // shards_of).reshape([-1 if axis == axis_at else 1 for axis in range(len(dims))])
    return loudness


def bell_draw(own_key, shape, scale, bound, split=(), held_as=jnp.bfloat16):
    values = scale * jax.random.normal(own_key, shape, jnp.float32)
    if split:
        values = values * block_scale(own_key, shape, split, -0.22, 0.18)
    return jnp.clip(values, -bound, bound).astype(held_as)


def setup_inputs(seed: int = 0) -> dict:
    streams_of = jax.random.split(jax.random.key(seed), 6)
    return {
        "bins": with_ends(jax.random.randint(streams_of[0], (F, ROWS), 0, BINS), jax.random.fold_in(streams_of[0], 1), 0, BINS - 1).astype(jnp.int32),
        "fold": with_ends(jax.random.randint(streams_of[1], (ROWS,), 0, FOLDS), jax.random.fold_in(streams_of[1], 1), 0, FOLDS - 1).astype(jnp.int32),
        "nodes": with_ends(jax.random.randint(streams_of[2], (ROWS, FOLDS), 0, NODES), jax.random.fold_in(streams_of[2], 1), 0, NODES - 1).astype(jnp.int32),
        "gradient": bell_draw(streams_of[3], (ROWS,), 1.0, 6.0, ((0, 8),)),
        "hessian": jnp.clip(jnp.exp(math.log(1.0) - 2.9996462 * jax.random.uniform(streams_of[4], (ROWS,), jnp.float32) ** block_scale(streams_of[4], (ROWS,), ((0, 8),), -0.2, 0.2)), 0.049804688, 1.0).astype(jnp.bfloat16),
    }


def reference(bins, fold, nodes, gradient, hessian):
    count = bins.shape[1]
    grad = gradient.astype(jnp.float32)[:, None]
    hess = hessian.astype(jnp.float32)[:, None]
    kept = (fold[:, None] != jnp.arange(FOLDS, dtype=jnp.int32)[None, :])[:, :, None]
    node_hot = nodes[:, :, None] == jnp.arange(NODES, dtype=jnp.int32)[None, None, :]
    selected = (node_hot & kept).reshape(count, FOLDS * NODES).astype(jnp.float32)
    weights = jnp.stack([grad * selected, hess * selected], axis=2).reshape(count, FOLDS * NODES * 2)

    def one_feature(column):
        return jax.ops.segment_sum(weights, column.astype(jnp.int32), num_segments=BINS)

    hist = lax.map(one_feature, bins)
    train_hist = hist.transpose(2, 0, 1)
    paired = train_hist.reshape(FOLDS, NODES, 2, F, BINS)
    totals = jnp.sum(paired[:, :, :, 0, :], axis=-1)
    left = jnp.cumsum(paired, axis=-1)[..., :BINS - 1]
    left_g, left_h = left[:, :, 0], left[:, :, 1]
    whole_g = totals[:, :, 0][:, :, None, None]
    whole_h = totals[:, :, 1][:, :, None, None]
    gain = left_g * left_g / (left_h + 1.0) + (whole_g - left_g) ** 2 / (whole_h - left_h + 1.0) - whole_g * whole_g / (whole_h + 1.0)
    node_gain = jnp.max(gain, axis=(2, 3))
    return train_hist, node_gain
```

```python
import functools

import jax
import jax.numpy as jnp
from jax import lax
from jax.experimental import pallas as pl
from jax.experimental.pallas import tpu as pltpu
from jax.sharding import PartitionSpec as P

BINS = 256
FOLDS = 10
NODES = 4
COLS = FOLDS * NODES * 2
X = 4
Y = 2
OWN = COLS // (X * Y)
NF = 4
BLK = OWN * NF
CUT = 24
F8 = jnp.float8_e4m3fn
MESH = pl.DeviceIdType.MESH
LOW = -1e30
LANES = 128
HALVES = BINS // LANES
KC = 512


def build_weights(fold_ref, nodes_ref, grad_ref, hess_ref, w_ref):
    rows = w_ref.shape[1]
    grad = grad_ref[...].astype(jnp.float32)
    hess = hess_ref[...].astype(jnp.float32)
    biggest = jnp.max(jnp.abs(grad), axis=1, keepdims=True)
    up = jnp.full((1, 1), 64.0, jnp.float32)
    down = jnp.full((1, 1), 1.0 / 64.0, jnp.float32)
    for e in (32, 16, 8, 4, 2, 1):
        fits = biggest * up * (2.0**e) <= 448.0
        up = jnp.where(fits, up * (2.0**e), up)
        down = jnp.where(fits, down * (2.0**-e), down)
    line = lax.broadcasted_iota(jnp.int32, (8, KC), 0)
    for at in range(0, rows, KC):
        g = grad[:, at : at + KC] * up
        h = hess[:, at : at + KC] * 256.0
        both = jnp.where(line % 2 == 0, jnp.broadcast_to(g, (8, KC)), jnp.broadcast_to(h, (8, KC)))
        first = both.astype(F8).astype(jnp.float32)
        second = (both - first) * 16.0
        fold = fold_ref[:, at : at + KC]
        pieces = [[], []]
        for k in range(FOLDS):
            node = nodes_ref[k : k + 1, at : at + KC]
            node = jnp.where(fold == k, -1, node)
            sel = jnp.broadcast_to(node, (8, KC)) == line // 2
            pieces[0].append(jnp.where(sel, first, 0.0))
            pieces[1].append(jnp.where(sel, second, 0.0))
        every = pieces[0] + pieces[1]
        for q in range(0, 2 * FOLDS, 4):
            w_ref[q * 8 : q * 8 + 32, at : at + KC] = jnp.concatenate(every[q : q + 4], axis=0).astype(F8)
    return down


def histogram(bins_ref, w_ref, loc_ref, slot, first, scale):
    rows = w_ref.shape[1]
    level = lax.broadcasted_iota(jnp.int32, (BINS, 1), 0).astype(jnp.float32).astype(jnp.bfloat16)
    for f in range(NF):
        total = None
        for at in range(0, rows, KC):
            b = bins_ref[pl.ds(first + f, 1), at : at + KC].astype(jnp.float32).astype(jnp.bfloat16)
            hot = jnp.where(b == level, jnp.bfloat16(1), jnp.bfloat16(0)).astype(F8)
            term = lax.dot_general(
                w_ref[:, at : at + KC], hot, (((1,), (1,)), ((), ())), preferred_element_type=jnp.float32
            )
            total = term if total is None else total + term
        hist = (total[:COLS] + total[COLS:] * (1.0 / 16.0)) * scale
        for part in range(HALVES):
            loc_ref[slot, part, pl.ds(f, COLS, stride=NF), :] = hist[:, part * LANES : (part + 1) * LANES]


def gains(done):
    lane = lax.broadcasted_iota(jnp.int32, (BLK, BINS), 1)
    line = lax.broadcasted_iota(jnp.int32, (BLK, BINS), 0)
    left = done
    step = 1
    while step < BINS:
        left = left + jnp.where(lane >= step, pltpu.roll(left, step, 1), 0.0)
        step *= 2
    whole = jnp.broadcast_to(left[:, BINS - 1 :], (BLK, BINS))
    left_h = pltpu.roll(left, BLK - NF, 0)
    whole_h = pltpu.roll(whole, BLK - NF, 0)
    good = (line % (2 * NF) < NF) & (lane < BINS - 1)
    left_h = jnp.where(good, left_h, 0.0)
    whole_h = jnp.where(good, whole_h, 0.0)
    gain = (
        left * left / (left_h + 1.0)
        + (whole - left) * (whole - left) / (whole_h - left_h + 1.0)
        - whole * whole / (whole_h + 1.0)
    )
    return jnp.where(good, gain, LOW)


def kernel(
    pairs, feats_way,
    bins_ref, fold_ref, nodes_ref, grad_ref, hess_ref,
    hist_ref, best_ref,
    w_ref, locx, locy, r1, r2, r3, y1, y2, y3, most, near_out, near_in, far_in,
    xs, xr, ys, yr, ns, nr, fs, fr,
):
    row = lax.axis_index("rows")
    feat = lax.axis_index("feat")
    y, x = row // X, row % X
    around = X * Y

    barrier = pltpu.get_barrier_semaphore()

    def greet_rows(d, c):
        pl.semaphore_signal(barrier, inc=1, device_id={"rows": (row + d) % around}, device_id_type=MESH)
        return c

    def greet_feats(d, c):
        pl.semaphore_signal(barrier, inc=1, device_id={"feat": (feat + d) % feats_way}, device_id_type=MESH)
        return c

    lax.fori_loop(1, around, greet_rows, 0)
    lax.fori_loop(1, feats_way, greet_feats, 0)

    right = {"rows": y * X + (x + 1) % X}
    left = {"rows": y * X + (x + X - 1) % X}
    over = {"rows": (Y - 1 - y) * X + x}

    def spot(yy, xx, start=0):
        return pl.multiple_of((yy * X + xx % X) * BLK + start, 8)

    def send(src, dst, sems, at, k, to):
        return pltpu.make_async_remote_copy(
            src_ref=src, dst_ref=dst, send_sem=sems[0].at[at, k], recv_sem=sems[1].at[at, k],
            device_id=to, device_id_type=MESH,
        )

    def x_copy(i, k):
        def blk(yy, xx):
            return locx.at[i, :, pl.ds(spot(yy, xx), BLK)]

        src, dst, to = (
            lambda: (blk(0, x + 2), r1.at[i, 0], right),
            lambda: (blk(1, x + 2), r1.at[i, 1], left),
            lambda: (blk(1, x + 1), r2.at[i, 1], right),
            lambda: (blk(0, x + 3), r2.at[i, 2], left),
            lambda: (blk(0, x + 1), r2.at[i, 0], right),
            lambda: (blk(1, x + 3), r2.at[i, 3], left),
            lambda: (blk(Y - 1 - y, x), r3.at[i], over),
        )[k]()
        return send(src, dst, (xs, xr), i, k, to)

    def y_copy(i, k):
        def part(xx, a, b):
            return locy.at[i, :, pl.ds(spot(y, xx, a), b - a)]

        def into(ref, a, b):
            return ref.at[:, pl.ds(a, b - a)]

        src, dst, to = (
            lambda: (locy.at[i, :, pl.ds(spot(Y - 1 - y, 0), X * BLK)], y1.at[i], over),
            lambda: (part(x + 2, 0, CUT), into(y2.at[i], 0, CUT), right),
            lambda: (part(x + 2, CUT, BLK), into(y2.at[i], CUT, BLK), left),
            lambda: (part(x + 1, CUT, BLK), into(y3.at[i, 0], CUT, BLK), right),
            lambda: (part(x + 3, 0, CUT), into(y3.at[i, 1], 0, CUT), left),
            lambda: (part(x + 1, 0, CUT), into(y3.at[i, 0], 0, CUT), right),
            lambda: (part(x + 3, CUT, BLK), into(y3.at[i, 1], CUT, BLK), left),
        )[k]()
        return send(src, dst, (ys, yr), i, k, to)

    down = build_weights(fold_ref, nodes_ref, grad_ref, hess_ref, w_ref)
    column = lax.broadcasted_iota(jnp.int32, (COLS, BINS), 0)
    scale = jnp.where(column % 2 == 0, jnp.broadcast_to(down, (COLS, BINS)), 1.0 / 256.0)
    most[...] = jnp.full(most.shape, LOW, jnp.float32)

    def visit(i, carry):
        @pl.when(i < pairs)
        def _():
            histogram(bins_ref, w_ref, locx, i, 2 * NF * i, scale)

            @pl.when(i == 0)
            def _():
                pl.semaphore_wait(barrier, around - 1 + feats_way - 1)

            for k in range(4):
                x_copy(i, k).start()
            histogram(bins_ref, w_ref, locy, i, 2 * NF * i + NF, scale)
            y_copy(i, 0).start()

        @pl.when((i >= 1) & (i < pairs + 1))
        def _():
            j = i - 1
            x_copy(j, 0).wait_recv()
            x_copy(j, 1).wait_recv()
            locx[j, :, pl.ds(spot(0, x + 1), BLK), :] += r1[j, 0]
            locx[j, :, pl.ds(spot(1, x + 3), BLK), :] += r1[j, 1]
            x_copy(j, 4).start()
            x_copy(j, 5).start()
            y_copy(j, 0).wait_recv()
            locy[j, :, pl.ds(spot(y, 0), X * BLK), :] += y1[j]
            for k in range(1, 5):
                y_copy(j, k).start()

        @pl.when((i >= 2) & (i < pairs + 2))
        def _():
            j = i - 2
            for k in range(2, 6):
                x_copy(j, k).wait_recv()
            locx[j, :, pl.ds(spot(0, x), BLK), :] += r2[j, 0] + r2[j, 2]
            locx[j, :, pl.ds(spot(1, x), BLK), :] += r2[j, 1] + r2[j, 3]
            x_copy(j, 6).start()
            y_copy(j, 1).wait_recv()
            y_copy(j, 2).wait_recv()
            locy[j, :, pl.ds(spot(y, x + 1), CUT), :] += y2[j, :, pl.ds(0, CUT), :]
            locy[j, :, pl.ds(spot(y, x + 3, CUT), BLK - CUT), :] += y2[j, :, pl.ds(CUT, BLK - CUT), :]
            y_copy(j, 5).start()
            y_copy(j, 6).start()

        @pl.when(i >= 3)
        def _():
            j = i - 3
            x_copy(j, 6).wait_recv()
            done_x = locx[j, :, pl.ds(spot(y, x), BLK), :] + r3[j]
            for k in range(3, 7):
                y_copy(j, k).wait_recv()
            done_y = locy[j, :, pl.ds(spot(y, x), BLK), :] + y3[j, 0] + y3[j, 1]
            done_x = jnp.concatenate([done_x[h] for h in range(HALVES)], axis=1)
            done_y = jnp.concatenate([done_y[h] for h in range(HALVES)], axis=1)
            for c in range(OWN):
                hist_ref[c, pl.ds(pl.multiple_of(2 * NF * j, 2 * NF), 2 * NF), :] = jnp.concatenate(
                    [done_x[c * NF : (c + 1) * NF], done_y[c * NF : (c + 1) * NF]], axis=0
                )
            most[...] = jnp.maximum(most[...], jnp.maximum(gains(done_x), gains(done_y)))

        return carry

    lax.fori_loop(0, pairs + 3, visit, 0)

    def settle(i, carry):
        for k in range(7):
            x_copy(i, k).wait_send()
            y_copy(i, k).wait_send()
        return carry

    lane = lax.broadcasted_iota(jnp.int32, (8, 128), 1)
    mine = jnp.full((8, 128), LOW, jnp.float32)
    for m in range(OWN // 2):
        part = most[m * 2 * NF : (m + 1) * 2 * NF, :]
        part = jnp.max(jnp.max(part, axis=1, keepdims=True), axis=0, keepdims=True)
        mine = jnp.where(lane == row * (OWN // 2) + m, jnp.broadcast_to(part, (8, 128)), mine)
    near_out[0] = mine

    def near(d):
        return pltpu.make_async_remote_copy(
            src_ref=near_out.at[0], dst_ref=near_in.at[d], send_sem=ns.at[d], recv_sem=nr.at[d],
            device_id={"feat": (feat + d) % feats_way}, device_id_type=MESH,
        )

    def far(d):
        return pltpu.make_async_remote_copy(
            src_ref=near_out.at[1], dst_ref=far_in.at[d], send_sem=fs.at[d], recv_sem=fr.at[d],
            device_id={"rows": (row + d) % around}, device_id_type=MESH,
        )

    for d in range(1, feats_way):
        near(d).start()
    lax.fori_loop(0, pairs, settle, 0)
    for d in range(1, feats_way):
        near(d).wait_recv()
        mine = jnp.maximum(mine, near_in[d])
    near_out[1] = mine
    for d in range(1, around):
        far(d).start()
    for d in range(1, around):
        far(d).wait_recv()
        mine = jnp.maximum(mine, far_in[d])
    for k in range(FOLDS):
        best_ref[k : k + 1, :] = mine[0:1, k * NODES : (k + 1) * NODES]
    for d in range(1, feats_way):
        near(d).wait_send()
    for d in range(1, around):
        far(d).wait_send()


def on_device(bins, fold, nodes, gradient, hessian):
    feats, rows_here = bins.shape
    pairs = feats // (2 * NF)
    feats_way = lax.axis_size("feat")
    around = X * Y
    f32 = jnp.float32
    dma = pltpu.SemaphoreType.DMA
    vmem = pl.BlockSpec(memory_space=pltpu.VMEM)
    return pl.pallas_call(
        functools.partial(kernel, pairs, feats_way),
        out_shape=(
            jax.ShapeDtypeStruct((OWN, feats, BINS), f32),
            jax.ShapeDtypeStruct((FOLDS, NODES), f32),
        ),
        in_specs=[vmem] * 5,
        out_specs=(vmem, vmem),
        scratch_shapes=[
            pltpu.VMEM((2 * COLS, rows_here), F8),
            pltpu.VMEM((pairs, HALVES, COLS * NF, LANES), f32),
            pltpu.VMEM((pairs, HALVES, COLS * NF, LANES), f32),
            pltpu.VMEM((pairs, 2, HALVES, BLK, LANES), f32),
            pltpu.VMEM((pairs, 4, HALVES, BLK, LANES), f32),
            pltpu.VMEM((pairs, HALVES, BLK, LANES), f32),
            pltpu.VMEM((pairs, HALVES, X * BLK, LANES), f32),
            pltpu.VMEM((pairs, HALVES, BLK, LANES), f32),
            pltpu.VMEM((pairs, 2, HALVES, BLK, LANES), f32),
            pltpu.VMEM((BLK, BINS), f32),
            pltpu.VMEM((2, 8, 128), f32),
            pltpu.VMEM((feats_way, 8, 128), f32),
            pltpu.VMEM((around, 8, 128), f32),
            dma((pairs, 7)), dma((pairs, 7)), dma((pairs, 7)), dma((pairs, 7)),
            dma((feats_way,)), dma((feats_way,)), dma((around,)), dma((around,)),
        ],
        compiler_params=pltpu.CompilerParams(
            collective_id=0, has_side_effects=True, vmem_limit_bytes=48 << 20
        ),
    )(bins, fold.reshape(1, -1), nodes.T, gradient.reshape(1, -1), hessian.reshape(1, -1))


def solution(mesh):
    in_specs = (P("feat", "rows"), P("rows"), P("rows", None), P("rows"), P("rows"))
    out_specs = (P("rows", "feat", None), P())
    return jax.shard_map(
        on_device, mesh=mesh, in_specs=in_specs, out_specs=out_specs, check_vma=False
    )
```

```python
import functools

import jax
import jax.numpy as jnp
from jax import lax
from jax.experimental import pallas as pl
from jax.experimental.pallas import tpu as pltpu
from jax.sharding import PartitionSpec as P

BINS = 256
FOLDS = 10
NODES = 4
COLS = FOLDS * NODES * 2
X = 4
Y = 2
OWN = COLS // (X * Y)
NF = 4
BLK = OWN * NF
CUT = 24
F8 = jnp.float8_e4m3fn
MESH = pl.DeviceIdType.MESH
LOW = -1e30
LANES = 128
HALVES = BINS // LANES
KC = 512


def build_weights(fold_ref, nodes_ref, grad_ref, hess_ref, w_ref):
    rows = w_ref.shape[1]
    line = lax.broadcasted_iota(jnp.int32, (8, KC), 0)
    for at in range(0, rows, KC):
        grad = jnp.broadcast_to(grad_ref[:, at : at + KC].astype(jnp.float32), (8, KC))
        hess = jnp.broadcast_to(hess_ref[:, at : at + KC].astype(jnp.float32), (8, KC))
        both = jnp.where(line % 2 == 0, grad, hess)
        fold = fold_ref[:, at : at + KC]
        made = []
        for k in range(FOLDS):
            node = jnp.where(fold == k, -1, nodes_ref[k : k + 1, at : at + KC])
            made.append(jnp.where(jnp.broadcast_to(node, (8, KC)) == line // 2, both, 0.0))
        for q in range(0, FOLDS, 2):
            w_ref[q * 8 : q * 8 + 16, at : at + KC] = jnp.concatenate(made[q : q + 2], axis=0).astype(jnp.bfloat16)


def histogram(bins_ref, w_ref, loc_ref, slot, first):
    rows = w_ref.shape[1]
    level = lax.broadcasted_iota(jnp.int32, (BINS, 1), 0).astype(jnp.float32).astype(jnp.bfloat16)
    for f in range(NF):
        total = None
        for at in range(0, rows, KC):
            b = bins_ref[pl.ds(first + f, 1), at : at + KC].astype(jnp.float32).astype(jnp.bfloat16)
            hot = jnp.where(b == level, jnp.bfloat16(1), jnp.bfloat16(0)).astype(F8)
            term = lax.dot_general(
                w_ref[:, at : at + KC], hot, (((1,), (1,)), ((), ())), preferred_element_type=jnp.float32
            )
            total = term if total is None else total + term
        for part in range(HALVES):
            loc_ref[slot, part, pl.ds(f, COLS, stride=NF), :] = total[:, part * LANES : (part + 1) * LANES]


def gains(done):
    lane = lax.broadcasted_iota(jnp.int32, (BLK, BINS), 1)
    line = lax.broadcasted_iota(jnp.int32, (BLK, BINS), 0)
    left = done
    step = 1
    while step < BINS:
        left = left + jnp.where(lane >= step, pltpu.roll(left, step, 1), 0.0)
        step *= 2
    whole = jnp.broadcast_to(left[:, BINS - 1 :], (BLK, BINS))
    left_h = pltpu.roll(left, BLK - NF, 0)
    whole_h = pltpu.roll(whole, BLK - NF, 0)
    good = (line % (2 * NF) < NF) & (lane < BINS - 1)
    left_h = jnp.where(good, left_h, 0.0)
    whole_h = jnp.where(good, whole_h, 0.0)
    gain = (
        left * left / (left_h + 1.0)
        + (whole - left) * (whole - left) / (whole_h - left_h + 1.0)
        - whole * whole / (whole_h + 1.0)
    )
    return jnp.where(good, gain, LOW)


def kernel(
    pairs, feats_way,
    bins_ref, fold_ref, nodes_ref, grad_ref, hess_ref,
    hist_ref, best_ref,
    w_ref, locx, locy, r1, r2, r3, y1, y2, y3, most, near_out, near_in, far_in,
    xs, xr, ys, yr, ns, nr, fs, fr,
):
    row = lax.axis_index("rows")
    feat = lax.axis_index("feat")
    y, x = row // X, row % X
    around = X * Y

    barrier = pltpu.get_barrier_semaphore()

    def greet_rows(d, c):
        pl.semaphore_signal(barrier, inc=1, device_id={"rows": (row + d) % around}, device_id_type=MESH)
        return c

    def greet_feats(d, c):
        pl.semaphore_signal(barrier, inc=1, device_id={"feat": (feat + d) % feats_way}, device_id_type=MESH)
        return c

    lax.fori_loop(1, around, greet_rows, 0)
    lax.fori_loop(1, feats_way, greet_feats, 0)

    right = {"rows": y * X + (x + 1) % X}
    left = {"rows": y * X + (x + X - 1) % X}
    over = {"rows": (Y - 1 - y) * X + x}

    def spot(yy, xx, start=0):
        return pl.multiple_of((yy * X + xx % X) * BLK + start, 8)

    def send(src, dst, sems, at, k, to):
        return pltpu.make_async_remote_copy(
            src_ref=src, dst_ref=dst, send_sem=sems[0].at[at, k], recv_sem=sems[1].at[at, k],
            device_id=to, device_id_type=MESH,
        )

    def x_copy(i, k):
        def blk(yy, xx):
            return locx.at[i, :, pl.ds(spot(yy, xx), BLK)]

        src, dst, to = (
            lambda: (blk(0, x + 2), r1.at[i, 0], right),
            lambda: (blk(1, x + 2), r1.at[i, 1], left),
            lambda: (blk(1, x + 1), r2.at[i, 1], right),
            lambda: (blk(0, x + 3), r2.at[i, 2], left),
            lambda: (blk(0, x + 1), r2.at[i, 0], right),
            lambda: (blk(1, x + 3), r2.at[i, 3], left),
            lambda: (blk(Y - 1 - y, x), r3.at[i], over),
        )[k]()
        return send(src, dst, (xs, xr), i, k, to)

    def y_copy(i, k):
        def part(xx, a, b):
            return locy.at[i, :, pl.ds(spot(y, xx, a), b - a)]

        def into(ref, a, b):
            return ref.at[:, pl.ds(a, b - a)]

        src, dst, to = (
            lambda: (locy.at[i, :, pl.ds(spot(Y - 1 - y, 0), X * BLK)], y1.at[i], over),
            lambda: (part(x + 2, 0, CUT), into(y2.at[i], 0, CUT), right),
            lambda: (part(x + 2, CUT, BLK), into(y2.at[i], CUT, BLK), left),
            lambda: (part(x + 1, CUT, BLK), into(y3.at[i, 0], CUT, BLK), right),
            lambda: (part(x + 3, 0, CUT), into(y3.at[i, 1], 0, CUT), left),
            lambda: (part(x + 1, 0, CUT), into(y3.at[i, 0], 0, CUT), right),
            lambda: (part(x + 3, CUT, BLK), into(y3.at[i, 1], CUT, BLK), left),
        )[k]()
        return send(src, dst, (ys, yr), i, k, to)

    build_weights(fold_ref, nodes_ref, grad_ref, hess_ref, w_ref)
    most[...] = jnp.full(most.shape, LOW, jnp.float32)

    def visit(i, carry):
        @pl.when(i < pairs)
        def _():
            histogram(bins_ref, w_ref, locx, i, 2 * NF * i)

            @pl.when(i == 0)
            def _():
                pl.semaphore_wait(barrier, around - 1 + feats_way - 1)

            for k in range(4):
                x_copy(i, k).start()
            histogram(bins_ref, w_ref, locy, i, 2 * NF * i + NF)
            y_copy(i, 0).start()

        @pl.when((i >= 1) & (i < pairs + 1))
        def _():
            j = i - 1
            x_copy(j, 0).wait_recv()
            x_copy(j, 1).wait_recv()
            locx[j, :, pl.ds(spot(0, x + 1), BLK), :] += r1[j, 0]
            locx[j, :, pl.ds(spot(1, x + 3), BLK), :] += r1[j, 1]
            x_copy(j, 4).start()
            x_copy(j, 5).start()
            y_copy(j, 0).wait_recv()
            locy[j, :, pl.ds(spot(y, 0), X * BLK), :] += y1[j]
            for k in range(1, 5):
                y_copy(j, k).start()

        @pl.when((i >= 2) & (i < pairs + 2))
        def _():
            j = i - 2
            for k in range(2, 6):
                x_copy(j, k).wait_recv()
            locx[j, :, pl.ds(spot(0, x), BLK), :] += r2[j, 0] + r2[j, 2]
            locx[j, :, pl.ds(spot(1, x), BLK), :] += r2[j, 1] + r2[j, 3]
            x_copy(j, 6).start()
            y_copy(j, 1).wait_recv()
            y_copy(j, 2).wait_recv()
            locy[j, :, pl.ds(spot(y, x + 1), CUT), :] += y2[j, :, pl.ds(0, CUT), :]
            locy[j, :, pl.ds(spot(y, x + 3, CUT), BLK - CUT), :] += y2[j, :, pl.ds(CUT, BLK - CUT), :]
            y_copy(j, 5).start()
            y_copy(j, 6).start()

        @pl.when(i >= 3)
        def _():
            j = i - 3
            x_copy(j, 6).wait_recv()
            done_x = locx[j, :, pl.ds(spot(y, x), BLK), :] + r3[j]
            for k in range(3, 7):
                y_copy(j, k).wait_recv()
            done_y = locy[j, :, pl.ds(spot(y, x), BLK), :] + y3[j, 0] + y3[j, 1]
            done_x = jnp.concatenate([done_x[h] for h in range(HALVES)], axis=1)
            done_y = jnp.concatenate([done_y[h] for h in range(HALVES)], axis=1)
            for c in range(OWN):
                hist_ref[c, pl.ds(pl.multiple_of(2 * NF * j, 2 * NF), 2 * NF), :] = jnp.concatenate(
                    [done_x[c * NF : (c + 1) * NF], done_y[c * NF : (c + 1) * NF]], axis=0
                )
            most[...] = jnp.maximum(most[...], jnp.maximum(gains(done_x), gains(done_y)))

        return carry

    lax.fori_loop(0, pairs + 3, visit, 0)

    def settle(i, carry):
        for k in range(7):
            x_copy(i, k).wait_send()
            y_copy(i, k).wait_send()
        return carry

    lane = lax.broadcasted_iota(jnp.int32, (8, 128), 1)
    mine = jnp.full((8, 128), LOW, jnp.float32)
    for m in range(OWN // 2):
        part = most[m * 2 * NF : (m + 1) * 2 * NF, :]
        part = jnp.max(jnp.max(part, axis=1, keepdims=True), axis=0, keepdims=True)
        mine = jnp.where(lane == row * (OWN // 2) + m, jnp.broadcast_to(part, (8, 128)), mine)
    near_out[0] = mine

    def near(d):
        return pltpu.make_async_remote_copy(
            src_ref=near_out.at[0], dst_ref=near_in.at[d], send_sem=ns.at[d], recv_sem=nr.at[d],
            device_id={"feat": (feat + d) % feats_way}, device_id_type=MESH,
        )

    def far(d):
        return pltpu.make_async_remote_copy(
            src_ref=near_out.at[1], dst_ref=far_in.at[d], send_sem=fs.at[d], recv_sem=fr.at[d],
            device_id={"rows": (row + d) % around}, device_id_type=MESH,
        )

    for d in range(1, feats_way):
        near(d).start()
    lax.fori_loop(0, pairs, settle, 0)
    for d in range(1, feats_way):
        near(d).wait_recv()
        mine = jnp.maximum(mine, near_in[d])
    near_out[1] = mine
    for d in range(1, around):
        far(d).start()
    for d in range(1, around):
        far(d).wait_recv()
        mine = jnp.maximum(mine, far_in[d])
    for k in range(FOLDS):
        best_ref[k : k + 1, :] = mine[0:1, k * NODES : (k + 1) * NODES]
    for d in range(1, feats_way):
        near(d).wait_send()
    for d in range(1, around):
        far(d).wait_send()


def on_device(bins, fold, nodes, gradient, hessian):
    feats, rows_here = bins.shape
    pairs = feats // (2 * NF)
    feats_way = lax.axis_size("feat")
    around = X * Y
    f32 = jnp.float32
    dma = pltpu.SemaphoreType.DMA
    vmem = pl.BlockSpec(memory_space=pltpu.VMEM)
    return pl.pallas_call(
        functools.partial(kernel, pairs, feats_way),
        out_shape=(
            jax.ShapeDtypeStruct((OWN, feats, BINS), f32),
            jax.ShapeDtypeStruct((FOLDS, NODES), f32),
        ),
        in_specs=[vmem] * 5,
        out_specs=(vmem, vmem),
        scratch_shapes=[
            pltpu.VMEM((COLS, rows_here), jnp.bfloat16),
            pltpu.VMEM((pairs, HALVES, COLS * NF, LANES), f32),
            pltpu.VMEM((pairs, HALVES, COLS * NF, LANES), f32),
            pltpu.VMEM((pairs, 2, HALVES, BLK, LANES), f32),
            pltpu.VMEM((pairs, 4, HALVES, BLK, LANES), f32),
            pltpu.VMEM((pairs, HALVES, BLK, LANES), f32),
            pltpu.VMEM((pairs, HALVES, X * BLK, LANES), f32),
            pltpu.VMEM((pairs, HALVES, BLK, LANES), f32),
            pltpu.VMEM((pairs, 2, HALVES, BLK, LANES), f32),
            pltpu.VMEM((BLK, BINS), f32),
            pltpu.VMEM((2, 8, 128), f32),
            pltpu.VMEM((feats_way, 8, 128), f32),
            pltpu.VMEM((around, 8, 128), f32),
            dma((pairs, 7)), dma((pairs, 7)), dma((pairs, 7)), dma((pairs, 7)),
            dma((feats_way,)), dma((feats_way,)), dma((around,)), dma((around,)),
        ],
        compiler_params=pltpu.CompilerParams(
            collective_id=0, has_side_effects=True, vmem_limit_bytes=48 << 20
        ),
    )(bins, fold.reshape(1, -1), nodes.T, gradient.reshape(1, -1), hessian.reshape(1, -1))


def solution(mesh):
    in_specs = (P("feat", "rows"), P("rows"), P("rows", None), P("rows"), P("rows"))
    out_specs = (P("rows", "feat", None), P())
    return jax.shard_map(
        on_device, mesh=mesh, in_specs=in_specs, out_specs=out_specs, check_vma=False
    )
```

```python
import functools

import jax
import jax.numpy as jnp
from jax import lax
from jax.experimental import pallas as pl
from jax.experimental.pallas import tpu as pltpu
from jax.sharding import PartitionSpec as P

BINS = 256
FOLDS = 10
NODES = 4
COLS = FOLDS * NODES * 2
X = 4
Y = 2
OWN = COLS // (X * Y)
NF = 4
BLK = OWN * NF
CUT = 24
F8 = jnp.float8_e4m3fn
MESH = pl.DeviceIdType.MESH
LOW = -1e30
LANES = 128
HALVES = BINS // LANES
KC = 512
KINDS = "xxxxxxxxgggg"
LAGS = {"x": (3, 6, 9), "y": (5, 7, 8), "g": (3,)}


def chosen(nodes, grad, hess):
    line = lax.broadcasted_iota(jnp.int32, (8, LANES), 0)
    both = jnp.where(line % 2 == 0, jnp.broadcast_to(grad, (8, LANES)), jnp.broadcast_to(hess, (8, LANES)))
    which = (line // 2).astype(nodes[0].dtype)
    return [jnp.where(jnp.broadcast_to(node, (8, LANES)) == which, both, 0.0) for node in nodes]


def build_weights(y, fold_ref, nodes_ref, grad_ref, hess_ref, w_ref, half_ref, letter_ref):
    grads = grad_ref[...].astype(jnp.float32)
    hesses = hess_ref[...].astype(jnp.float32)
    some = FOLDS // Y
    for j in range(w_ref.shape[1] // LANES):
        at = slice(j * LANES, (j + 1) * LANES)
        grad, hess, fold = grads[j : j + 1], hesses[j : j + 1], fold_ref[j : j + 1, :]

        nodes = [jnp.where(fold == k, -1, nodes_ref[k : k + 1, at]) for k in range(FOLDS)]
        made = chosen(nodes, grad, hess)
        for q in range(0, FOLDS, 2):
            w_ref[q * 8 : q * 8 + 16, at] = jnp.concatenate(made[q : q + 2], axis=0).astype(jnp.bfloat16)
        made = [jnp.where(y == 0, made[i], made[some + i]) for i in range(some)]
        half_ref[0, :, at] = jnp.concatenate(made, axis=0).astype(jnp.bfloat16)
        for i in range(some):
            letter_ref[i : i + 1, at] = jnp.where(y == 0, nodes[some + i], nodes[i]).astype(jnp.float32)
        letter_ref[some : some + 1, at] = grad
        letter_ref[some + 1 : some + 2, at] = hess


def read_letter(letter_ref, half_ref):
    some = FOLDS // Y
    for j in range(letter_ref.shape[1] // LANES):
        at = slice(j * LANES, (j + 1) * LANES)
        nodes = [letter_ref[i : i + 1, at] for i in range(some)]
        made = chosen(nodes, letter_ref[some : some + 1, at], letter_ref[some + 1 : some + 2, at])
        half_ref[1, :, at] = jnp.concatenate(made, axis=0).astype(jnp.bfloat16)


def histogram(parts, into_ref):
    level = lax.broadcasted_iota(jnp.int32, (BINS, 1), 0).astype(jnp.float32).astype(jnp.bfloat16)

    def one(f, carry):
        total = None
        for bins_ref, first, w_ref in parts:
            for at in range(0, w_ref.shape[1], KC):
                b = bins_ref[pl.ds(first + f, 1), at : at + KC].astype(jnp.float32).astype(jnp.bfloat16)
                hot = jnp.where(b == level, jnp.bfloat16(1), jnp.bfloat16(0)).astype(F8)
                term = lax.dot_general(
                    w_ref[:, at : at + KC], hot, (((1,), (1,)), ((), ())), preferred_element_type=jnp.float32
                )
                total = term if total is None else total + term
        for half in range(HALVES):
            into_ref[half, pl.ds(f, total.shape[0], stride=NF), :] = total[:, half * LANES : (half + 1) * LANES]
        return carry

    lax.fori_loop(0, NF, one, 0)


def gains(done):
    lane = lax.broadcasted_iota(jnp.int32, (BLK, BINS), 1)
    line = lax.broadcasted_iota(jnp.int32, (BLK, BINS), 0)
    left = done
    step = 1
    while step < BINS:
        left = left + jnp.where(lane >= step, pltpu.roll(left, step, 1), 0.0)
        step *= 2
    whole = jnp.broadcast_to(left[:, BINS - 1 :], (BLK, BINS))
    left_h = pltpu.roll(left, BLK - NF, 0)
    whole_h = pltpu.roll(whole, BLK - NF, 0)
    good = (line % (2 * NF) < NF) & (lane < BINS - 1)
    left_h = jnp.where(good, left_h, 0.0)
    whole_h = jnp.where(good, whole_h, 0.0)
    gain = (
        left * left / (left_h + 1.0)
        + (whole - left) * (whole - left) / (whole_h - left_h + 1.0)
        - whole * whole / (whole_h + 1.0)
    )
    return jnp.where(good, gain, LOW)


def plan(chunks):
    counts = {"x": 0, "y": 0, "g": 0}
    order, events = [], []
    alone = len(KINDS) - KINDS.count("g")
    for c, kind in enumerate(KINDS):
        place = alone + counts["g"] if kind == "g" else counts["x"] + counts["y"]
        order.append((kind, counts[kind], place * NF))
        counts[kind] += 1
        for step, lag in enumerate(LAGS[kind]):
            events.append((c + lag, c, step + 1))
    return order, sorted(events), counts


def kernel(
    feats, feats_way,
    bins_hbm, fold_hbm, nodes_hbm, grad_hbm, hess_hbm,
    hist_ref, best_ref,
    bins_ref, fold_ref, nodes_ref, grad_ref, hess_ref,
    w_ref, half_ref, letter_out, letter_in, bins_in, loc, r1, r2, r3, y1, y2, y3, rg, most, mine_ref, core_in, near_in, far_in,
    get, ps, pr, es, er, cs, cr, ns, nr, fs, fr,
):
    row = lax.axis_index("rows")
    feat = lax.axis_index("feat")
    y, x = row // X, row % X
    around = X * Y
    chips = feats_way // 2
    chip, core = feat // 2, feat % 2
    order, events, _ = plan(feats // NF)

    barrier = pltpu.get_barrier_semaphore()

    def to_row(d):
        return {"rows": (row + d) % around}

    def to_chip(d):
        return {"feat": (chip + d) % chips * 2 + core}

    to_core = {"feat": chip * 2 + 1 - core}
    for d in range(1, around):
        pl.semaphore_signal(barrier, inc=1, device_id=to_row(d), device_id_type=MESH)
    for d in range(1, chips):
        pl.semaphore_signal(barrier, inc=1, device_id=to_chip(d), device_id_type=MESH)
    pl.semaphore_signal(barrier, inc=1, device_id=to_core, device_id_type=MESH)

    pairs = ((nodes_hbm, nodes_ref), (fold_hbm, fold_ref), (grad_hbm, grad_ref), (hess_hbm, hess_ref), (bins_hbm, bins_ref))
    gets = [pltpu.make_async_copy(src, dst, get.at[i]) for i, (src, dst) in enumerate(pairs)]
    for g in gets:
        g.start()

    right = {"rows": y * X + (x + 1) % X}
    left = {"rows": y * X + (x + X - 1) % X}
    over = {"rows": (Y - 1 - y) * X + x}

    def spot(yy, xx, start=0):
        return pl.multiple_of((yy * X + xx % X) * BLK + start, 8)

    def send(src, dst, sems, k, to):
        return pltpu.make_async_remote_copy(
            src_ref=src, dst_ref=dst, send_sem=sems[0].at[k], recv_sem=sems[1].at[k],
            device_id=to, device_id_type=MESH,
        )

    def rows_of(c, at, size):
        return loc.at[c, :, pl.ds(at, size)]

    def copy(c, k):
        kind, i, base = order[c]

        def part(yy, xx, a=0, b=BLK):
            return rows_of(c, spot(yy, xx, a), b - a)

        def cut(ref, a, b):
            return ref.at[:, pl.ds(a, b - a)]

        if kind == "g":
            there = (x + k + 1) % X
            src = rows_of(c, pl.multiple_of(there * BLK, 8), BLK)
            return send(src, rg.at[i, k], (ps.at[c], pr.at[c]), k, {"rows": y * X + there})
        if kind == "x":
            src, dst, to = (
                lambda: (part(0, x + 2), r1.at[i, 0], right),
                lambda: (part(1, x + 2), r1.at[i, 1], left),
                lambda: (part(1, x + 1), r2.at[i, 1], right),
                lambda: (part(0, x + 3), r2.at[i, 2], left),
                lambda: (part(0, x + 1), r2.at[i, 0], right),
                lambda: (part(1, x + 3), r2.at[i, 3], left),
                lambda: (part(Y - 1 - y, x), r3.at[i], over),
            )[k]()
        else:
            src, dst, to = (
                lambda: (rows_of(c, spot(Y - 1 - y, 0), X * BLK), y1.at[i], over),
                lambda: (part(y, x + 2, 0, CUT), cut(y2.at[i], 0, CUT), right),
                lambda: (part(y, x + 2, CUT, BLK), cut(y2.at[i], CUT, BLK), left),
                lambda: (part(y, x + 1, CUT, BLK), cut(y3.at[i, 0], CUT, BLK), right),
                lambda: (part(y, x + 3, 0, CUT), cut(y3.at[i, 1], 0, CUT), left),
                lambda: (part(y, x + 1, 0, CUT), cut(y3.at[i, 0], 0, CUT), right),
                lambda: (part(y, x + 3, CUT, BLK), cut(y3.at[i, 1], CUT, BLK), left),
            )[k]()
        return send(src, dst, (ps.at[c], pr.at[c]), k, to)

    def start(c, ks):
        for k in ks:
            copy(c, k).start()

    def arrive(c, ks):
        for k in ks:
            copy(c, k).wait_recv()

    def grow(c, at, size, *terms):
        total = terms[0]
        for term in terms[1:]:
            total = total + term
        loc[c, :, pl.ds(at, size), :] += total

    def finish(c, *terms):
        kind, i, base = order[c]
        at = pl.multiple_of(x * BLK, 8) if kind == "g" else spot(y, x)
        done = loc[c, :, pl.ds(at, BLK), :]
        for term in terms:
            done = done + term
        done = jnp.concatenate([done[half] for half in range(HALVES)], axis=1)
        for col in range(OWN):
            hist_ref[col, base : base + NF, :] = done[col * NF : (col + 1) * NF]
        most[...] = jnp.maximum(most[...], gains(done))

    def advance(c, step):
        kind, i, base = order[c]
        if kind == "g":
            arrive(c, range(X - 1))
            finish(c, *[rg[i, d] for d in range(X - 1)])
        elif kind == "x" and step == 1:
            arrive(c, (0, 1))
            grow(c, spot(0, x + 1), BLK, r1[i, 0])
            grow(c, spot(1, x + 3), BLK, r1[i, 1])
            start(c, (2, 3, 4, 5))
        elif kind == "x" and step == 2:
            arrive(c, (2, 3, 4, 5))
            grow(c, spot(Y - 1 - y, x), BLK, r2[i, Y - 1 - y], r2[i, Y + Y - 1 - y])
            start(c, (6,))
            grow(c, spot(y, x), BLK, r2[i, y], r2[i, Y + y])
        elif kind == "x":
            arrive(c, (6,))
            finish(c, r3[i])
        elif step == 1:
            arrive(c, (0,))
            grow(c, spot(y, 0), X * BLK, y1[i])
            start(c, (1, 2))
        elif step == 2:
            arrive(c, (1, 2))
            grow(c, spot(y, x + 1), CUT, y2[i, :, pl.ds(0, CUT), :])
            grow(c, spot(y, x + 3, CUT), BLK - CUT, y2[i, :, pl.ds(CUT, BLK - CUT), :])
            start(c, (3, 4, 5, 6))
        else:
            arrive(c, (3, 4, 5, 6))
            finish(c, y3[i, 0], y3[i, 1])

    for g in gets[:4]:
        g.wait()
    build_weights(y, fold_ref, nodes_ref, grad_ref, hess_ref, w_ref, half_ref, letter_out)
    most[...] = jnp.full(most.shape, LOW, jnp.float32)
    gets[4].wait()

    shared = (len(KINDS) - KINDS.count("g")) * NF
    swaps = [send(letter_out, letter_in, (es, er), 0, over)]
    for i in range((feats - shared) // 8):
        swaps.append(
            send(bins_ref.at[pl.ds(shared + 8 * i, 8)], bins_in.at[pl.ds(8 * i, 8)], (es, er), i + 1, over)
        )
    todo = list(events)
    for c, (kind, i, base) in enumerate(order):
        if kind == "g" and i == 0:
            swaps[0].wait_recv()
            read_letter(letter_in, half_ref)
        if kind == "g" and i % 2 == 0:
            swaps[1 + i // 2].wait_recv()
        if kind == "g":
            histogram(((bins_ref, base, half_ref.at[0]), (bins_in, i * NF, half_ref.at[1])), loc.at[c])
        else:
            histogram(((bins_ref, base, w_ref),), loc.at[c])
        if c == 0:
            pl.semaphore_wait(barrier, around - 1 + chips - 1 + 1)
            for e in swaps:
                e.start()
        start(c, {"x": (0, 1), "y": (0,), "g": range(X - 1)}[kind])
        while todo and todo[0][0] <= c:
            advance(*todo.pop(0)[1:])
    for _, c, step in todo:
        advance(c, step)

    lane = lax.broadcasted_iota(jnp.int32, (1, LANES), 1)
    mine = jnp.full((1, LANES), LOW, jnp.float32)
    for m in range(OWN // 2):
        part = most[m * 2 * NF : (m + 1) * 2 * NF, :]
        part = jnp.max(jnp.max(part, axis=1, keepdims=True), axis=0, keepdims=True)
        mine = jnp.where(lane == row * (OWN // 2) + m, jnp.broadcast_to(part, (1, LANES)), mine)

    mine_ref[0] = mine
    swap = send(mine_ref.at[0], core_in.at[0], (cs, cr), 0, to_core)
    swap.start()
    swap.wait_recv()
    mine = jnp.maximum(mine, core_in[0])
    mine_ref[1] = mine
    near = [send(mine_ref.at[1], near_in.at[d], (ns, nr), d, to_chip(d)) for d in range(1, chips)]
    for n in near:
        n.start()
    for c, (kind, i, base) in enumerate(order):
        for k in range(X - 1 if kind == "g" else 7):
            copy(c, k).wait_send()
    for n in near:
        n.wait_recv()
    for d in range(1, chips):
        mine = jnp.maximum(mine, near_in[d])
    mine_ref[2] = mine
    far = [send(mine_ref.at[2], far_in.at[d], (fs, fr), d, to_row(d)) for d in range(1, around)]
    for n in far:
        n.start()
    for n in far:
        n.wait_recv()
    for d in range(1, around):
        mine = jnp.maximum(mine, far_in[d])
    for k in range(FOLDS):
        best_ref[k : k + 1, :] = mine[0:1, k * NODES : (k + 1) * NODES]
    for n in [swap] + swaps + near + far:
        n.wait_send()


def on_device(bins, fold, nodes, gradient, hessian):
    feats, rows_here = bins.shape
    chunks = feats // NF
    counts = plan(chunks)[2]
    feats_way = lax.axis_size("feat")
    around = X * Y
    f32 = jnp.float32
    dma = pltpu.SemaphoreType.DMA
    vmem = pl.BlockSpec(memory_space=pltpu.VMEM)
    stay = pl.BlockSpec(memory_space=pltpu.HBM)
    lines = rows_here // LANES
    return pl.pallas_call(
        functools.partial(kernel, feats, feats_way),
        out_shape=(
            jax.ShapeDtypeStruct((OWN, feats, BINS), f32),
            jax.ShapeDtypeStruct((FOLDS, NODES), f32),
        ),
        in_specs=[stay] * 5,
        out_specs=(vmem, vmem),
        scratch_shapes=[
            pltpu.VMEM((feats, rows_here), jnp.int32),
            pltpu.VMEM((lines, LANES), jnp.int32),
            pltpu.VMEM((FOLDS, rows_here), jnp.int32),
            pltpu.VMEM((lines, LANES), jnp.bfloat16),
            pltpu.VMEM((lines, LANES), jnp.bfloat16),
            pltpu.VMEM((COLS, rows_here), jnp.bfloat16),
            pltpu.VMEM((2, COLS // Y, rows_here), jnp.bfloat16),
            pltpu.VMEM((8, rows_here), f32),
            pltpu.VMEM((8, rows_here), f32),
            pltpu.VMEM((counts["g"] * NF, rows_here), jnp.int32),
            pltpu.VMEM((chunks, HALVES, COLS * NF, LANES), f32),
            pltpu.VMEM((max(counts["x"], 1), 2, HALVES, BLK, LANES), f32),
            pltpu.VMEM((max(counts["x"], 1), 4, HALVES, BLK, LANES), f32),
            pltpu.VMEM((max(counts["x"], 1), HALVES, BLK, LANES), f32),
            pltpu.VMEM((max(counts["y"], 1), HALVES, X * BLK, LANES), f32),
            pltpu.VMEM((max(counts["y"], 1), HALVES, BLK, LANES), f32),
            pltpu.VMEM((max(counts["y"], 1), 2, HALVES, BLK, LANES), f32),
            pltpu.VMEM((counts["g"], X - 1, HALVES, BLK, LANES), f32),
            pltpu.VMEM((BLK, BINS), f32),
            pltpu.VMEM((3, 1, LANES), f32),
            pltpu.VMEM((1, 1, LANES), f32),
            pltpu.VMEM((feats_way // 2, 1, LANES), f32),
            pltpu.VMEM((around, 1, LANES), f32),
            dma((5,)),
            dma((chunks, 7)), dma((chunks, 7)),
            dma((1 + chunks // 2,)), dma((1 + chunks // 2,)),
            dma((1,)), dma((1,)),
            dma((feats_way // 2,)), dma((feats_way // 2,)),
            dma((around,)), dma((around,)),
        ],
        compiler_params=pltpu.CompilerParams(
            collective_id=0, has_side_effects=True, vmem_limit_bytes=48 << 20
        ),
    )(*[
        pltpu.with_memory_space_constraint(a, pltpu.HBM)
        for a in (bins, fold.reshape(lines, LANES), nodes.T, gradient.reshape(lines, LANES), hessian.reshape(lines, LANES))
    ])


def solution(mesh):
    in_specs = (P("feat", "rows"), P("rows"), P("rows", None), P("rows"), P("rows"))
    out_specs = (P("rows", "feat", None), P())
    return jax.shard_map(
        on_device, mesh=mesh, in_specs=in_specs, out_specs=out_specs, check_vma=False
    )
```

```python
import functools

import jax
import jax.numpy as jnp
from jax import lax
from jax.experimental import pallas as pl
from jax.experimental.pallas import tpu as pltpu
from jax.sharding import PartitionSpec as P

BINS = 256
FOLDS = 10
NODES = 4
COLS = FOLDS * NODES * 2
X = 4
Y = 2
OWN = COLS // (X * Y)
NF = 4
BLK = OWN * NF
CUT = 24
F8 = jnp.float8_e4m3fn
MESH = pl.DeviceIdType.MESH
LOW = -1e30
LANES = 128
HALVES = BINS // LANES
KC = 512
KINDS = "xxxxxxxxgggg"
LAGS = {"x": (3, 6, 9), "y": (5, 7, 8), "g": (3,)}


def chosen(nodes, grad, hess):
    line = lax.broadcasted_iota(jnp.int32, (8, LANES), 0)
    both = jnp.where(line % 2 == 0, jnp.broadcast_to(grad, (8, LANES)), jnp.broadcast_to(hess, (8, LANES)))
    which = (line // 2).astype(nodes[0].dtype)
    return [jnp.where(jnp.broadcast_to(node, (8, LANES)) == which, both, 0.0) for node in nodes]


def build_weights(y, fold_ref, nodes_ref, grad_ref, hess_ref, w_ref, half_ref, letter_ref):
    grads = grad_ref[...].astype(jnp.float32)
    hesses = hess_ref[...].astype(jnp.float32)
    some = FOLDS // Y
    for j in range(w_ref.shape[1] // LANES):
        at = slice(j * LANES, (j + 1) * LANES)
        grad, hess, fold = grads[j : j + 1], hesses[j : j + 1], fold_ref[j : j + 1, :]

        nodes = [jnp.where(fold == k, -1, nodes_ref[k : k + 1, at]) for k in range(FOLDS)]
        made = chosen(nodes, grad, hess)
        for q in range(0, FOLDS, 2):
            w_ref[q * 8 : q * 8 + 16, at] = jnp.concatenate(made[q : q + 2], axis=0).astype(jnp.bfloat16)
        made = [jnp.where(y == 0, made[i], made[some + i]) for i in range(some)]
        half_ref[0, :, at] = jnp.concatenate(made, axis=0).astype(jnp.bfloat16)
        for i in range(some):
            letter_ref[i : i + 1, at] = jnp.where(y == 0, nodes[some + i], nodes[i]).astype(jnp.float32)
        letter_ref[some : some + 1, at] = grad
        letter_ref[some + 1 : some + 2, at] = hess


def read_letter(letter_ref, half_ref):
    some = FOLDS // Y
    for j in range(letter_ref.shape[1] // LANES):
        at = slice(j * LANES, (j + 1) * LANES)
        nodes = [letter_ref[i : i + 1, at] for i in range(some)]
        made = chosen(nodes, letter_ref[some : some + 1, at], letter_ref[some + 1 : some + 2, at])
        half_ref[1, :, at] = jnp.concatenate(made, axis=0).astype(jnp.bfloat16)


def histogram(parts, into_ref):
    level = lax.broadcasted_iota(jnp.int32, (BINS, 1), 0).astype(jnp.float32).astype(jnp.bfloat16)

    def one(f, carry):
        total = None
        for bins_ref, first, w_ref in parts:
            for at in range(0, w_ref.shape[1], KC):
                b = bins_ref[pl.ds(first + f, 1), at : at + KC].astype(jnp.float32).astype(jnp.bfloat16)
                hot = jnp.where(b == level, jnp.bfloat16(1), jnp.bfloat16(0)).astype(F8)
                term = lax.dot_general(
                    w_ref[:, at : at + KC], hot, (((1,), (1,)), ((), ())), preferred_element_type=jnp.float32
                )
                total = term if total is None else total + term
        for half in range(HALVES):
            into_ref[half, pl.ds(f, total.shape[0], stride=NF), :] = total[:, half * LANES : (half + 1) * LANES]
        return carry

    lax.fori_loop(0, NF, one, 0, unroll=4)


def gains(done):
    lane = lax.broadcasted_iota(jnp.int32, (BLK, BINS), 1)
    line = lax.broadcasted_iota(jnp.int32, (BLK, BINS), 0)
    left = done
    step = 1
    while step < BINS:
        left = left + jnp.where(lane >= step, pltpu.roll(left, step, 1), 0.0)
        step *= 2
    whole = jnp.broadcast_to(left[:, BINS - 1 :], (BLK, BINS))
    left_h = pltpu.roll(left, BLK - NF, 0)
    whole_h = pltpu.roll(whole, BLK - NF, 0)
    good = (line % (2 * NF) < NF) & (lane < BINS - 1)
    left_h = jnp.where(good, left_h, 0.0)
    whole_h = jnp.where(good, whole_h, 0.0)
    gain = (
        left * left / (left_h + 1.0)
        + (whole - left) * (whole - left) / (whole_h - left_h + 1.0)
        - whole * whole / (whole_h + 1.0)
    )
    return jnp.where(good, gain, LOW)


def plan(chunks):
    counts = {"x": 0, "y": 0, "g": 0}
    order, events = [], []
    alone = len(KINDS) - KINDS.count("g")
    for c, kind in enumerate(KINDS):
        place = alone + counts["g"] if kind == "g" else counts["x"] + counts["y"]
        order.append((kind, counts[kind], place * NF))
        counts[kind] += 1
        for step, lag in enumerate(LAGS[kind]):
            events.append((c + lag, c, step + 1))
    return order, sorted(events), counts


def kernel(
    feats, feats_way,
    bins_hbm, fold_hbm, nodes_hbm, grad_hbm, hess_hbm,
    hist_ref, best_ref,
    bins_ref, fold_ref, nodes_ref, grad_ref, hess_ref,
    w_ref, half_ref, letter_out, letter_in, bins_in, loc, r1, r2, r3, y1, y2, y3, rg, most, mine_ref, core_in, near_in, far_in,
    get, ps, pr, es, er, cs, cr, ns, nr, fs, fr,
):
    row = lax.axis_index("rows")
    feat = lax.axis_index("feat")
    y, x = row // X, row % X
    around = X * Y
    chips = feats_way // 2
    chip, core = feat // 2, feat % 2
    order, events, _ = plan(feats // NF)

    barrier = pltpu.get_barrier_semaphore()

    def to_row(d):
        return {"rows": (row + d) % around}

    def to_chip(d):
        return {"feat": (chip + d) % chips * 2 + core}

    to_core = {"feat": chip * 2 + 1 - core}
    for d in range(1, around):
        pl.semaphore_signal(barrier, inc=1, device_id=to_row(d), device_id_type=MESH)
    for d in range(1, chips):
        pl.semaphore_signal(barrier, inc=1, device_id=to_chip(d), device_id_type=MESH)
    pl.semaphore_signal(barrier, inc=1, device_id=to_core, device_id_type=MESH)

    pairs = ((nodes_hbm, nodes_ref), (fold_hbm, fold_ref), (grad_hbm, grad_ref), (hess_hbm, hess_ref), (bins_hbm, bins_ref))
    gets = [pltpu.make_async_copy(src, dst, get.at[i]) for i, (src, dst) in enumerate(pairs)]
    for g in gets:
        g.start()

    right = {"rows": y * X + (x + 1) % X}
    left = {"rows": y * X + (x + X - 1) % X}
    over = {"rows": (Y - 1 - y) * X + x}

    def spot(yy, xx, start=0):
        return pl.multiple_of((yy * X + xx % X) * BLK + start, 8)

    def send(src, dst, sems, k, to):
        return pltpu.make_async_remote_copy(
            src_ref=src, dst_ref=dst, send_sem=sems[0].at[k], recv_sem=sems[1].at[k],
            device_id=to, device_id_type=MESH,
        )

    def rows_of(c, at, size):
        return loc.at[c, :, pl.ds(at, size)]

    def copy(c, k):
        kind, i, base = order[c]

        def part(yy, xx, a=0, b=BLK):
            return rows_of(c, spot(yy, xx, a), b - a)

        def cut(ref, a, b):
            return ref.at[:, pl.ds(a, b - a)]

        if kind == "g":
            there = (x + k + 1) % X
            src = rows_of(c, pl.multiple_of(there * BLK, 8), BLK)
            return send(src, rg.at[i, k], (ps.at[c], pr.at[c]), k, {"rows": y * X + there})
        if kind == "x":
            src, dst, to = (
                lambda: (part(0, x + 2), r1.at[i, 0], right),
                lambda: (part(1, x + 2), r1.at[i, 1], left),
                lambda: (part(1, x + 1), r2.at[i, 1], right),
                lambda: (part(0, x + 3), r2.at[i, 2], left),
                lambda: (part(0, x + 1), r2.at[i, 0], right),
                lambda: (part(1, x + 3), r2.at[i, 3], left),
                lambda: (part(Y - 1 - y, x), r3.at[i], over),
            )[k]()
        else:
            src, dst, to = (
                lambda: (rows_of(c, spot(Y - 1 - y, 0), X * BLK), y1.at[i], over),
                lambda: (part(y, x + 2, 0, CUT), cut(y2.at[i], 0, CUT), right),
                lambda: (part(y, x + 2, CUT, BLK), cut(y2.at[i], CUT, BLK), left),
                lambda: (part(y, x + 1, CUT, BLK), cut(y3.at[i, 0], CUT, BLK), right),
                lambda: (part(y, x + 3, 0, CUT), cut(y3.at[i, 1], 0, CUT), left),
                lambda: (part(y, x + 1, 0, CUT), cut(y3.at[i, 0], 0, CUT), right),
                lambda: (part(y, x + 3, CUT, BLK), cut(y3.at[i, 1], CUT, BLK), left),
            )[k]()
        return send(src, dst, (ps.at[c], pr.at[c]), k, to)

    def start(c, ks):
        for k in ks:
            copy(c, k).start()

    def arrive(c, ks):
        for k in ks:
            copy(c, k).wait_recv()

    def grow(c, at, size, *terms):
        total = terms[0]
        for term in terms[1:]:
            total = total + term
        loc[c, :, pl.ds(at, size), :] += total

    def finish(c, *terms):
        kind, i, base = order[c]
        at = pl.multiple_of(x * BLK, 8) if kind == "g" else spot(y, x)
        done = loc[c, :, pl.ds(at, BLK), :]
        for term in terms:
            done = done + term
        done = jnp.concatenate([done[half] for half in range(HALVES)], axis=1)
        for col in range(OWN):
            hist_ref[col, base : base + NF, :] = done[col * NF : (col + 1) * NF]
        most[...] = jnp.maximum(most[...], gains(done))

    def advance(c, step):
        kind, i, base = order[c]
        if kind == "g":
            arrive(c, range(X - 1))
            finish(c, *[rg[i, d] for d in range(X - 1)])
        elif kind == "x" and step == 1:
            arrive(c, (0, 1))
            grow(c, spot(0, x + 1), BLK, r1[i, 0])
            grow(c, spot(1, x + 3), BLK, r1[i, 1])
            start(c, (2, 3, 4, 5))
        elif kind == "x" and step == 2:
            arrive(c, (2, 3, 4, 5))
            grow(c, spot(Y - 1 - y, x), BLK, r2[i, Y - 1 - y], r2[i, Y + Y - 1 - y])
            start(c, (6,))
            grow(c, spot(y, x), BLK, r2[i, y], r2[i, Y + y])
        elif kind == "x":
            arrive(c, (6,))
            finish(c, r3[i])
        elif step == 1:
            arrive(c, (0,))
            grow(c, spot(y, 0), X * BLK, y1[i])
            start(c, (1, 2))
        elif step == 2:
            arrive(c, (1, 2))
            grow(c, spot(y, x + 1), CUT, y2[i, :, pl.ds(0, CUT), :])
            grow(c, spot(y, x + 3, CUT), BLK - CUT, y2[i, :, pl.ds(CUT, BLK - CUT), :])
            start(c, (3, 4, 5, 6))
        else:
            arrive(c, (3, 4, 5, 6))
            finish(c, y3[i, 0], y3[i, 1])

    for g in gets[:4]:
        g.wait()
    build_weights(y, fold_ref, nodes_ref, grad_ref, hess_ref, w_ref, half_ref, letter_out)
    most[...] = jnp.full(most.shape, LOW, jnp.float32)
    gets[4].wait()

    shared = (len(KINDS) - KINDS.count("g")) * NF
    swaps = [send(letter_out, letter_in, (es, er), 0, over)]
    for i in range((feats - shared) // 8):
        swaps.append(
            send(bins_ref.at[pl.ds(shared + 8 * i, 8)], bins_in.at[pl.ds(8 * i, 8)], (es, er), i + 1, over)
        )
    todo = list(events)
    for c, (kind, i, base) in enumerate(order):
        if kind == "g" and i == 0:
            swaps[0].wait_recv()
            read_letter(letter_in, half_ref)
        if kind == "g" and i % 2 == 0:
            swaps[1 + i // 2].wait_recv()
        if kind == "g":
            histogram(((bins_ref, base, half_ref.at[0]), (bins_in, i * NF, half_ref.at[1])), loc.at[c])
        else:
            histogram(((bins_ref, base, w_ref),), loc.at[c])
        if c == 0:
            pl.semaphore_wait(barrier, around - 1 + chips - 1 + 1)
            for e in swaps:
                e.start()
        start(c, {"x": (0, 1), "y": (0,), "g": range(X - 1)}[kind])
        while todo and todo[0][0] <= c:
            advance(*todo.pop(0)[1:])
    for _, c, step in todo:
        advance(c, step)

    lane = lax.broadcasted_iota(jnp.int32, (1, LANES), 1)
    mine = jnp.full((1, LANES), LOW, jnp.float32)
    for m in range(OWN // 2):
        part = most[m * 2 * NF : (m + 1) * 2 * NF, :]
        part = jnp.max(jnp.max(part, axis=1, keepdims=True), axis=0, keepdims=True)
        mine = jnp.where(lane == row * (OWN // 2) + m, jnp.broadcast_to(part, (1, LANES)), mine)

    mine_ref[0] = mine
    swap = send(mine_ref.at[0], core_in.at[0], (cs, cr), 0, to_core)
    swap.start()
    swap.wait_recv()
    mine = jnp.maximum(mine, core_in[0])
    mine_ref[1] = mine
    near = [send(mine_ref.at[1], near_in.at[d], (ns, nr), d, to_chip(d)) for d in range(1, chips)]
    for n in near:
        n.start()
    for c, (kind, i, base) in enumerate(order):
        for k in range(X - 1 if kind == "g" else 7):
            copy(c, k).wait_send()
    for n in near:
        n.wait_recv()
    for d in range(1, chips):
        mine = jnp.maximum(mine, near_in[d])
    mine_ref[2] = mine
    far = [send(mine_ref.at[2], far_in.at[d], (fs, fr), d, to_row(d)) for d in range(1, around)]
    for n in far:
        n.start()
    for n in far:
        n.wait_recv()
    for d in range(1, around):
        mine = jnp.maximum(mine, far_in[d])
    for k in range(FOLDS):
        best_ref[k : k + 1, :] = mine[0:1, k * NODES : (k + 1) * NODES]
    for n in [swap] + swaps + near + far:
        n.wait_send()


def on_device(bins, fold, nodes, gradient, hessian):
    feats, rows_here = bins.shape
    chunks = feats // NF
    counts = plan(chunks)[2]
    feats_way = lax.axis_size("feat")
    around = X * Y
    f32 = jnp.float32
    dma = pltpu.SemaphoreType.DMA
    vmem = pl.BlockSpec(memory_space=pltpu.VMEM)
    stay = pl.BlockSpec(memory_space=pltpu.HBM)
    lines = rows_here // LANES
    return pl.pallas_call(
        functools.partial(kernel, feats, feats_way),
        out_shape=(
            jax.ShapeDtypeStruct((OWN, feats, BINS), f32),
            jax.ShapeDtypeStruct((FOLDS, NODES), f32),
        ),
        in_specs=[stay] * 5,
        out_specs=(vmem, vmem),
        scratch_shapes=[
            pltpu.VMEM((feats, rows_here), jnp.int32),
            pltpu.VMEM((lines, LANES), jnp.int32),
            pltpu.VMEM((FOLDS, rows_here), jnp.int32),
            pltpu.VMEM((lines, LANES), jnp.bfloat16),
            pltpu.VMEM((lines, LANES), jnp.bfloat16),
            pltpu.VMEM((COLS, rows_here), jnp.bfloat16),
            pltpu.VMEM((2, COLS // Y, rows_here), jnp.bfloat16),
            pltpu.VMEM((8, rows_here), f32),
            pltpu.VMEM((8, rows_here), f32),
            pltpu.VMEM((counts["g"] * NF, rows_here), jnp.int32),
            pltpu.VMEM((chunks, HALVES, COLS * NF, LANES), f32),
            pltpu.VMEM((max(counts["x"], 1), 2, HALVES, BLK, LANES), f32),
            pltpu.VMEM((max(counts["x"], 1), 4, HALVES, BLK, LANES), f32),
            pltpu.VMEM((max(counts["x"], 1), HALVES, BLK, LANES), f32),
            pltpu.VMEM((max(counts["y"], 1), HALVES, X * BLK, LANES), f32),
            pltpu.VMEM((max(counts["y"], 1), HALVES, BLK, LANES), f32),
            pltpu.VMEM((max(counts["y"], 1), 2, HALVES, BLK, LANES), f32),
            pltpu.VMEM((counts["g"], X - 1, HALVES, BLK, LANES), f32),
            pltpu.VMEM((BLK, BINS), f32),
            pltpu.VMEM((3, 1, LANES), f32),
            pltpu.VMEM((1, 1, LANES), f32),
            pltpu.VMEM((feats_way // 2, 1, LANES), f32),
            pltpu.VMEM((around, 1, LANES), f32),
            dma((5,)),
            dma((chunks, 7)), dma((chunks, 7)),
            dma((1 + chunks // 2,)), dma((1 + chunks // 2,)),
            dma((1,)), dma((1,)),
            dma((feats_way // 2,)), dma((feats_way // 2,)),
            dma((around,)), dma((around,)),
        ],
        compiler_params=pltpu.CompilerParams(
            collective_id=0, has_side_effects=True, vmem_limit_bytes=48 << 20
        ),
    )(*[
        pltpu.with_memory_space_constraint(a, pltpu.HBM)
        for a in (bins, fold.reshape(lines, LANES), nodes.T, gradient.reshape(lines, LANES), hessian.reshape(lines, LANES))
    ])


def solution(mesh):
    in_specs = (P("feat", "rows"), P("rows"), P("rows", None), P("rows"), P("rows"))
    out_specs = (P("rows", "feat", None), P())
    return jax.shard_map(
        on_device, mesh=mesh, in_specs=in_specs, out_specs=out_specs, check_vma=False
    )
```

```python
import functools

import jax
import jax.numpy as jnp
from jax import lax
from jax.experimental import pallas as pl
from jax.experimental.pallas import tpu as pltpu
from jax.sharding import PartitionSpec as P

BINS = 256
FOLDS = 10
NODES = 4
COLS = FOLDS * NODES * 2
X = 4
Y = 2
OWN = COLS // (X * Y)
NF = 4
BLK = OWN * NF
CUT = 24
F8 = jnp.float8_e4m3fn
MESH = pl.DeviceIdType.MESH
LOW = -1e30
LANES = 128
HALVES = BINS // LANES
KC = 512
KINDS = "xxxxxxxxgggg"
LAGS = {"x": (3, 6, 9), "y": (5, 7, 8), "g": (3,)}


def chosen(nodes, grad, hess):
    line = lax.broadcasted_iota(jnp.int32, (8, LANES), 0)
    both = jnp.where(line % 2 == 0, jnp.broadcast_to(grad, (8, LANES)), jnp.broadcast_to(hess, (8, LANES)))
    which = (line // 2).astype(nodes[0].dtype)
    return [jnp.where(jnp.broadcast_to(node, (8, LANES)) == which, both, 0.0) for node in nodes]


def build_weights(y, fold_ref, nodes_ref, grad_ref, hess_ref, w_ref, half_ref, letter_ref):
    grads = grad_ref[...].astype(jnp.float32)
    hesses = hess_ref[...].astype(jnp.float32)
    some = FOLDS // Y
    for j in range(w_ref.shape[1] // LANES):
        at = slice(j * LANES, (j + 1) * LANES)
        grad, hess, fold = grads[j : j + 1], hesses[j : j + 1], fold_ref[j : j + 1, :]

        nodes = [jnp.where(fold == k, -1, nodes_ref[k : k + 1, at]) for k in range(FOLDS)]
        made = chosen(nodes, grad, hess)
        for q in range(0, FOLDS, 2):
            w_ref[q * 8 : q * 8 + 16, at] = jnp.concatenate(made[q : q + 2], axis=0).astype(jnp.bfloat16)
        made = [jnp.where(y == 0, made[i], made[some + i]) for i in range(some)]
        half_ref[0, :, at] = jnp.concatenate(made, axis=0).astype(jnp.bfloat16)
        for i in range(some):
            letter_ref[i : i + 1, at] = jnp.where(y == 0, nodes[some + i], nodes[i]).astype(jnp.float32)
        letter_ref[some : some + 1, at] = grad
        letter_ref[some + 1 : some + 2, at] = hess


def read_letter(letter_ref, half_ref):
    some = FOLDS // Y
    for j in range(letter_ref.shape[1] // LANES):
        at = slice(j * LANES, (j + 1) * LANES)
        nodes = [letter_ref[i : i + 1, at] for i in range(some)]
        made = chosen(nodes, letter_ref[some : some + 1, at], letter_ref[some + 1 : some + 2, at])
        half_ref[1, :, at] = jnp.concatenate(made, axis=0).astype(jnp.bfloat16)


def histogram(parts, into_ref):
    level = lax.broadcasted_iota(jnp.int32, (BINS, 1), 0).astype(jnp.float32).astype(jnp.bfloat16)

    def one(f, carry):
        total = None
        for bins_ref, first, w_ref in parts:
            for at in range(0, w_ref.shape[1], KC):
                b = bins_ref[pl.ds(first + f, 1), at : at + KC].astype(jnp.float32).astype(jnp.bfloat16)
                hot = jnp.where(b == level, jnp.bfloat16(1), jnp.bfloat16(0)).astype(F8)
                term = lax.dot_general(
                    w_ref[:, at : at + KC], hot, (((1,), (1,)), ((), ())), preferred_element_type=jnp.float32
                )
                total = term if total is None else total + term
        for half in range(HALVES):
            into_ref[half, pl.ds(f, total.shape[0], stride=NF), :] = total[:, half * LANES : (half + 1) * LANES]
        return carry

    lax.fori_loop(0, NF, one, 0, unroll=4)


def gains(done):
    lane = lax.broadcasted_iota(jnp.int32, (BLK, BINS), 1)
    line = lax.broadcasted_iota(jnp.int32, (BLK, BINS), 0)
    left = done
    step = 1
    while step < BINS:
        left = left + jnp.where(lane >= step, pltpu.roll(left, step, 1), 0.0)
        step *= 2
    whole = jnp.broadcast_to(left[:, BINS - 1 :], (BLK, BINS))
    left_h = pltpu.roll(left, BLK - NF, 0)
    whole_h = pltpu.roll(whole, BLK - NF, 0)
    good = (line % (2 * NF) < NF) & (lane < BINS - 1)
    left_h = jnp.where(good, left_h, 0.0)
    whole_h = jnp.where(good, whole_h, 0.0)
    gain = (
        left * left / (left_h + 1.0)
        + (whole - left) * (whole - left) / (whole_h - left_h + 1.0)
        - whole * whole / (whole_h + 1.0)
    )
    return jnp.where(good, gain, LOW)


def plan(chunks):
    counts = {"x": 0, "y": 0, "g": 0}
    order, events = [], []
    alone = len(KINDS) - KINDS.count("g")
    for c, kind in enumerate(KINDS):
        place = alone + counts["g"] if kind == "g" else counts["x"] + counts["y"]
        order.append((kind, counts[kind], place * NF))
        counts[kind] += 1
        for step, lag in enumerate(LAGS[kind]):
            events.append((c + lag, c, step + 1))
    return order, sorted(events), counts


def kernel(
    feats, feats_way,
    bins_hbm, fold_hbm, nodes_hbm, grad_hbm, hess_hbm,
    hist_ref, best_ref,
    bins_ref, fold_ref, nodes_ref, grad_ref, hess_ref,
    w_ref, half_ref, letter_out, letter_in, bins_in, loc, r1, r2, r3, y1, y2, y3, rg, most, mine_ref, core_in, near_in, far_in,
    get, ps, pr, es, er, cs, cr, ns, nr, fs, fr,
):
    row = lax.axis_index("rows")
    feat = lax.axis_index("feat")
    y, x = row // X, row % X
    around = X * Y
    chips = feats_way // 2
    chip, core = feat // 2, feat % 2
    order, events, _ = plan(feats // NF)

    barrier = pltpu.get_barrier_semaphore()

    def to_row(d):
        return {"rows": (row + d) % around}

    def to_chip(d):
        return {"feat": (chip + d) % chips * 2 + core}

    to_core = {"feat": chip * 2 + 1 - core}
    for d in range(1, around):
        pl.semaphore_signal(barrier, inc=1, device_id=to_row(d), device_id_type=MESH)
    for d in range(1, chips):
        pl.semaphore_signal(barrier, inc=1, device_id=to_chip(d), device_id_type=MESH)
    pl.semaphore_signal(barrier, inc=1, device_id=to_core, device_id_type=MESH)

    pairs = ((nodes_hbm, nodes_ref), (fold_hbm, fold_ref), (grad_hbm, grad_ref), (hess_hbm, hess_ref), (bins_hbm, bins_ref))
    gets = [pltpu.make_async_copy(src, dst, get.at[i]) for i, (src, dst) in enumerate(pairs)]
    for g in gets:
        g.start()

    right = {"rows": y * X + (x + 1) % X}
    left = {"rows": y * X + (x + X - 1) % X}
    over = {"rows": (Y - 1 - y) * X + x}

    def spot(yy, xx, start=0):
        return pl.multiple_of((yy * X + xx % X) * BLK + start, 8)

    def send(src, dst, sems, k, to):
        return pltpu.make_async_remote_copy(
            src_ref=src, dst_ref=dst, send_sem=sems[0].at[k], recv_sem=sems[1].at[k],
            device_id=to, device_id_type=MESH,
        )

    def rows_of(c, at, size):
        return loc.at[c, :, pl.ds(at, size)]

    def copy(c, k):
        kind, i, base = order[c]

        def part(yy, xx, a=0, b=BLK):
            return rows_of(c, spot(yy, xx, a), b - a)

        def cut(ref, a, b):
            return ref.at[:, pl.ds(a, b - a)]

        if kind == "g":
            there = (x + k + 1) % X
            src = rows_of(c, pl.multiple_of(there * BLK, 8), BLK)
            return send(src, rg.at[i, k], (ps.at[c], pr.at[c]), k, {"rows": y * X + there})
        if kind == "x":
            src, dst, to = (
                lambda: (part(0, x + 2), r1.at[i, 0], right),
                lambda: (part(1, x + 2), r1.at[i, 1], left),
                lambda: (part(1, x + 1), r2.at[i, 1], right),
                lambda: (part(0, x + 3), r2.at[i, 2], left),
                lambda: (part(0, x + 1), r2.at[i, 0], right),
                lambda: (part(1, x + 3), r2.at[i, 3], left),
                lambda: (part(Y - 1 - y, x), r3.at[i], over),
            )[k]()
        else:
            src, dst, to = (
                lambda: (rows_of(c, spot(Y - 1 - y, 0), X * BLK), y1.at[i], over),
                lambda: (part(y, x + 2, 0, CUT), cut(y2.at[i], 0, CUT), right),
                lambda: (part(y, x + 2, CUT, BLK), cut(y2.at[i], CUT, BLK), left),
                lambda: (part(y, x + 1, CUT, BLK), cut(y3.at[i, 0], CUT, BLK), right),
                lambda: (part(y, x + 3, 0, CUT), cut(y3.at[i, 1], 0, CUT), left),
                lambda: (part(y, x + 1, 0, CUT), cut(y3.at[i, 0], 0, CUT), right),
                lambda: (part(y, x + 3, CUT, BLK), cut(y3.at[i, 1], CUT, BLK), left),
            )[k]()
        return send(src, dst, (ps.at[c], pr.at[c]), k, to)

    def start(c, ks):
        for k in ks:
            copy(c, k).start()

    def arrive(c, ks):
        for k in ks:
            copy(c, k).wait_recv()

    def grow(c, at, size, *terms):
        total = terms[0]
        for term in terms[1:]:
            total = total + term
        loc[c, :, pl.ds(at, size), :] += total

    def finish(c, *terms):
        kind, i, base = order[c]
        at = pl.multiple_of(x * BLK, 8) if kind == "g" else spot(y, x)
        done = loc[c, :, pl.ds(at, BLK), :]
        for term in terms:
            done = done + term
        done = jnp.concatenate([done[half] for half in range(HALVES)], axis=1)
        for col in range(OWN):
            hist_ref[col, base : base + NF, :] = done[col * NF : (col + 1) * NF]
        most[...] = jnp.maximum(most[...], gains(done))

    def advance(c, step):
        kind, i, base = order[c]
        if kind == "g":
            arrive(c, range(X - 1))
            finish(c, *[rg[i, d] for d in range(X - 1)])
        elif kind == "x" and step == 1:
            arrive(c, (0, 1))
            grow(c, spot(0, x + 1), BLK, r1[i, 0])
            grow(c, spot(1, x + 3), BLK, r1[i, 1])
            start(c, (4, 5))
        elif kind == "x" and step == 2:
            arrive(c, (2, 3, 4, 5))
            grow(c, spot(Y - 1 - y, x), BLK, r2[i, Y - 1 - y], r2[i, Y + Y - 1 - y])
            start(c, (6,))
            grow(c, spot(y, x), BLK, r2[i, y], r2[i, Y + y])
        elif kind == "x":
            arrive(c, (6,))
            finish(c, r3[i])
        elif step == 1:
            arrive(c, (0,))
            grow(c, spot(y, 0), X * BLK, y1[i])
            start(c, (1, 2))
        elif step == 2:
            arrive(c, (1, 2))
            grow(c, spot(y, x + 1), CUT, y2[i, :, pl.ds(0, CUT), :])
            grow(c, spot(y, x + 3, CUT), BLK - CUT, y2[i, :, pl.ds(CUT, BLK - CUT), :])
            start(c, (3, 4, 5, 6))
        else:
            arrive(c, (3, 4, 5, 6))
            finish(c, y3[i, 0], y3[i, 1])

    for g in gets[:4]:
        g.wait()
    build_weights(y, fold_ref, nodes_ref, grad_ref, hess_ref, w_ref, half_ref, letter_out)
    most[...] = jnp.full(most.shape, LOW, jnp.float32)
    gets[4].wait()

    shared = (len(KINDS) - KINDS.count("g")) * NF
    swaps = [send(letter_out, letter_in, (es, er), 0, over)]
    for i in range((feats - shared) // 8):
        swaps.append(
            send(bins_ref.at[pl.ds(shared + 8 * i, 8)], bins_in.at[pl.ds(8 * i, 8)], (es, er), i + 1, over)
        )
    todo = list(events)
    for c, (kind, i, base) in enumerate(order):
        if kind == "g" and i == 0:
            swaps[0].wait_recv()
            read_letter(letter_in, half_ref)
        if kind == "g" and i % 2 == 0:
            swaps[1 + i // 2].wait_recv()
        if kind == "g":
            histogram(((bins_ref, base, half_ref.at[0]), (bins_in, i * NF, half_ref.at[1])), loc.at[c])
        else:
            histogram(((bins_ref, base, w_ref),), loc.at[c])
        if c == 0:
            pl.semaphore_wait(barrier, around - 1 + chips - 1 + 1)
            for e in swaps:
                e.start()
        start(c, {"x": (0, 1, 2, 3), "y": (0,), "g": range(X - 1)}[kind])
        while todo and todo[0][0] <= c:
            advance(*todo.pop(0)[1:])
    for _, c, step in todo:
        advance(c, step)

    lane = lax.broadcasted_iota(jnp.int32, (1, LANES), 1)
    mine = jnp.full((1, LANES), LOW, jnp.float32)
    for m in range(OWN // 2):
        part = most[m * 2 * NF : (m + 1) * 2 * NF, :]
        part = jnp.max(jnp.max(part, axis=1, keepdims=True), axis=0, keepdims=True)
        mine = jnp.where(lane == row * (OWN // 2) + m, jnp.broadcast_to(part, (1, LANES)), mine)

    mine_ref[0] = mine
    swap = send(mine_ref.at[0], core_in.at[0], (cs, cr), 0, to_core)
    swap.start()
    swap.wait_recv()
    mine = jnp.maximum(mine, core_in[0])
    mine_ref[1] = mine
    near = [send(mine_ref.at[1], near_in.at[d], (ns, nr), d, to_chip(d)) for d in range(1, chips)]
    for n in near:
        n.start()
    for c, (kind, i, base) in enumerate(order):
        for k in range(X - 1 if kind == "g" else 7):
            copy(c, k).wait_send()
    for n in near:
        n.wait_recv()
    for d in range(1, chips):
        mine = jnp.maximum(mine, near_in[d])
    mine_ref[2] = mine
    far = [send(mine_ref.at[2], far_in.at[d], (fs, fr), d, to_row(d)) for d in range(1, around)]
    for n in far:
        n.start()
    for n in far:
        n.wait_recv()
    for d in range(1, around):
        mine = jnp.maximum(mine, far_in[d])
    for k in range(FOLDS):
        best_ref[k : k + 1, :] = mine[0:1, k * NODES : (k + 1) * NODES]
    for n in [swap] + swaps + near + far:
        n.wait_send()


def on_device(bins, fold, nodes, gradient, hessian):
    feats, rows_here = bins.shape
    chunks = feats // NF
    counts = plan(chunks)[2]
    feats_way = lax.axis_size("feat")
    around = X * Y
    f32 = jnp.float32
    dma = pltpu.SemaphoreType.DMA
    vmem = pl.BlockSpec(memory_space=pltpu.VMEM)
    stay = pl.BlockSpec(memory_space=pltpu.HBM)
    lines = rows_here // LANES
    return pl.pallas_call(
        functools.partial(kernel, feats, feats_way),
        out_shape=(
            jax.ShapeDtypeStruct((OWN, feats, BINS), f32),
            jax.ShapeDtypeStruct((FOLDS, NODES), f32),
        ),
        in_specs=[stay] * 5,
        out_specs=(vmem, vmem),
        scratch_shapes=[
            pltpu.VMEM((feats, rows_here), jnp.int32),
            pltpu.VMEM((lines, LANES), jnp.int32),
            pltpu.VMEM((FOLDS, rows_here), jnp.int32),
            pltpu.VMEM((lines, LANES), jnp.bfloat16),
            pltpu.VMEM((lines, LANES), jnp.bfloat16),
            pltpu.VMEM((COLS, rows_here), jnp.bfloat16),
            pltpu.VMEM((2, COLS // Y, rows_here), jnp.bfloat16),
            pltpu.VMEM((8, rows_here), f32),
            pltpu.VMEM((8, rows_here), f32),
            pltpu.VMEM((counts["g"] * NF, rows_here), jnp.int32),
            pltpu.VMEM((chunks, HALVES, COLS * NF, LANES), f32),
            pltpu.VMEM((max(counts["x"], 1), 2, HALVES, BLK, LANES), f32),
            pltpu.VMEM((max(counts["x"], 1), 4, HALVES, BLK, LANES), f32),
            pltpu.VMEM((max(counts["x"], 1), HALVES, BLK, LANES), f32),
            pltpu.VMEM((max(counts["y"], 1), HALVES, X * BLK, LANES), f32),
            pltpu.VMEM((max(counts["y"], 1), HALVES, BLK, LANES), f32),
            pltpu.VMEM((max(counts["y"], 1), 2, HALVES, BLK, LANES), f32),
            pltpu.VMEM((counts["g"], X - 1, HALVES, BLK, LANES), f32),
            pltpu.VMEM((BLK, BINS), f32),
            pltpu.VMEM((3, 1, LANES), f32),
            pltpu.VMEM((1, 1, LANES), f32),
            pltpu.VMEM((feats_way // 2, 1, LANES), f32),
            pltpu.VMEM((around, 1, LANES), f32),
            dma((5,)),
            dma((chunks, 7)), dma((chunks, 7)),
            dma((1 + chunks // 2,)), dma((1 + chunks // 2,)),
            dma((1,)), dma((1,)),
            dma((feats_way // 2,)), dma((feats_way // 2,)),
            dma((around,)), dma((around,)),
        ],
        compiler_params=pltpu.CompilerParams(
            collective_id=0, has_side_effects=True, vmem_limit_bytes=48 << 20
        ),
    )(*[
        pltpu.with_memory_space_constraint(a, pltpu.HBM)
        for a in (bins, fold.reshape(lines, LANES), nodes.T, gradient.reshape(lines, LANES), hessian.reshape(lines, LANES))
    ])


def solution(mesh):
    in_specs = (P("feat", "rows"), P("rows"), P("rows", None), P("rows"), P("rows"))
    out_specs = (P("rows", "feat", None), P())
    return jax.shard_map(
        on_device, mesh=mesh, in_specs=in_specs, out_specs=out_specs, check_vma=False
    )
```
